32 devices in a mesh: tm: 4 (over z), space: 8 (over y, x, core).
Axes of the slice: x: 2, y: 2, z: 4, core: 2. Of those that a mesh axis runs over, the one named last changes fastest.
Arguments:
- queries: bfloat16 [4, 1024, 1120], P('tm', 'space'), may hold values from -6 to 6
- keys_in: bfloat16 [4, 1024, 1120], P('tm', 'space'), may hold values from -30 to 30
- values_in: bfloat16 [4, 1024, 1120], P('tm', 'space'), may hold values from -10 to 10
- grad_attn: bfloat16 [4, 1024, 1120], P('tm', 'space'), may hold values from -6 to 6
Outputs:
- mixed: bfloat16 [4, 1024, 1120], P('tm', 'space')
- grad_queries: bfloat16 [4, 1024, 1120], P('tm', 'space')
- grad_keys: bfloat16 [4, 1024, 1120], P('tm', 'space')
- values_gradient: bfloat16 [4, 1024, 1120], P('tm', 'space')
The draws below stay inside these ranges and needn't reach their ends.
All inputs are finite; a program needn't handle non-finite values.
Results may differ from the reference program's by a relative error of at most 0.001.
Values sent between devices are 32-bit elements; how exact they have to be, the bound alone decides.
A program may use at most 64 MiB of HBM per device.

```python
import jax
import jax.numpy as jnp
from jax import lax

HEADS = 10
HEAD_DIM = 112
C = 1120
GROUPS = 4
ROWS = 1024


def draw_keys_in(key, part):
    first, second = jax.random.split(jax.random.fold_in(key, 11))
    blocks = ROWS // 32
    scales = jnp.exp(jax.random.uniform(first, (GROUPS, blocks, 1, HEADS, 1), jnp.float32, jnp.log(0.3), jnp.log(3.0)))
    noise = jnp.clip(jax.random.normal(second, (GROUPS, blocks, 32, HEADS, HEAD_DIM), jnp.float32), -5.0, 5.0)
    return (noise * scales).reshape(GROUPS, ROWS, C).astype(jnp.bfloat16)


def draw_values_in(key, part):
    first, second = jax.random.split(jax.random.fold_in(key, 23))
    blocks = ROWS // 32
    means = jnp.clip(jax.random.normal(first, (GROUPS, blocks, 1, C), jnp.float32), -4.0, 4.0)
    noise = jnp.clip(jax.random.normal(second, (GROUPS, blocks, 32, C), jnp.float32), -4.0, 4.0)
    return (means + noise).reshape(GROUPS, ROWS, C).astype(jnp.bfloat16)


def block_scale(own_key, dims, cuts, low, largest):
    def one(dim, shards_of):
        steps = jax.random.uniform(jax.random.fold_in(jax.random.fold_in(own_key, 6), dim), (shards_of,), jnp.float32, low / len(cuts), largest / len(cuts))
        return jnp.repeat(jnp.exp(steps), dims[dim] // shards_of).reshape((-1,) + (1,) * (len(dims) - dim - 1))

    level = one(*cuts[0])
    for cut in cuts[1:]:
        level = level * one(*cut)
    return level


def centred(stream_key, dims, spread, bound, shards=(), kind=jnp.bfloat16):
    gain = block_scale(stream_key, dims, shards, -0.22, 0.18) if shards else 1.0
    entries = jax.random.normal(stream_key, dims, jnp.float32) * spread * gain
    return jnp.minimum(jnp.maximum(entries, -bound), bound).astype(kind)


def setup_inputs(seed: int = 0) -> dict:
    keys = jax.random.split(jax.random.key(seed), 5)
    queries = centred(keys[0], (GROUPS, ROWS, C), 1.0, 6.0, ((0, 4), (1, 8)))
    keys_in = draw_keys_in(jax.random.fold_in(keys[4], 71), 0)
    values_in = draw_values_in(jax.random.fold_in(keys[4], 71), 0)
    grad_attn = centred(keys[3], (GROUPS, ROWS, C), 1.0, 6.0, ((0, 4), (1, 8)))
    return dict(queries=queries, keys_in=keys_in, values_in=values_in, grad_attn=grad_attn)


HIGH_PRECISION = lax.Precision.HIGHEST


def reference(queries, keys_in, values_in, grad_attn):
    phi_q = jax.nn.relu(queries.astype(jnp.float32)).reshape(GROUPS, ROWS, HEADS, HEAD_DIM)
    phi_k = jax.nn.relu(keys_in.astype(jnp.float32)).reshape(GROUPS, ROWS, HEADS, HEAD_DIM)
    vals = values_in.astype(jnp.float32).reshape(GROUPS, ROWS, HEADS, HEAD_DIM)
    state_local = jnp.einsum("grhk,grhv->ghkv", phi_k, vals, precision=HIGH_PRECISION)
    total_local = jnp.sum(phi_k, axis=1)
    running_state = jnp.cumsum(state_local, axis=0)
    running_total = jnp.cumsum(total_local, axis=0)

    def forward_group(args):
        query_features, step_state, step_total = args
        numerator = jnp.einsum("igx,gxb->igb", query_features, step_state, precision=HIGH_PRECISION)
        denom = jnp.einsum("rhk,hk->rh", query_features, step_total, precision=HIGH_PRECISION) + 1.0
        return numerator / denom[..., None], denom

    attn_f, denom = lax.map(forward_group, (phi_q, running_state, running_total))
    mixed = attn_f.reshape(GROUPS, ROWS, C).astype(jnp.bfloat16)
    g_out = grad_attn.astype(jnp.float32).reshape(GROUPS, ROWS, HEADS, HEAD_DIM)

    def backward_group(args):
        query_features, go, af, dn, step_state, step_total = args
        numerator_gradient = go / dn[..., None]
        denominator_gradient = -jnp.sum(go * af, axis=-1) / dn
        feature_gradient = jnp.einsum("tqd,qwd->tqw", numerator_gradient, step_state, precision=HIGH_PRECISION) + denominator_gradient[..., None] * step_total[None]
        step_state_gradient = jnp.einsum("isp,isz->spz", query_features, numerator_gradient, precision=HIGH_PRECISION)
        gtt = jnp.einsum("rhk,rh->hk", query_features, denominator_gradient, precision=HIGH_PRECISION)
        return feature_gradient, step_state_gradient, gtt

    feature_gradient, gstate_local, gtotal_local = lax.map(backward_group, (phi_q, g_out, attn_f, denom, running_state, running_total))
    grad_queries = jnp.where(queries.reshape(GROUPS, ROWS, HEADS, HEAD_DIM) > 0, feature_gradient, 0.0)
    state_gradient = jnp.flip(jnp.cumsum(jnp.flip(gstate_local, 0), axis=0), 0)
    total_gradient = jnp.flip(jnp.cumsum(jnp.flip(gtotal_local, 0), axis=0), 0)

    def key_group(args):
        key_features, value_block, state_gradient_step, total_gradient_step = args
        value_gradient = jnp.einsum("igx,gxb->igb", key_features, state_gradient_step, precision=HIGH_PRECISION)
        key_gradient = jnp.einsum("tqd,qwd->tqw", value_block, state_gradient_step, precision=HIGH_PRECISION) + total_gradient_step[None]
        return value_gradient, key_gradient

    values_gradient, key_gradient = lax.map(key_group, (phi_k, vals, state_gradient, total_gradient))
    grad_keys = jnp.where(keys_in.reshape(GROUPS, ROWS, HEADS, HEAD_DIM) > 0, key_gradient, 0.0)
    return (mixed,
            grad_queries.reshape(GROUPS, ROWS, C).astype(jnp.bfloat16),
            grad_keys.reshape(GROUPS, ROWS, C).astype(jnp.bfloat16),
            values_gradient.reshape(GROUPS, ROWS, C).astype(jnp.bfloat16))
```

```python
import functools

import jax
import jax.numpy as jnp
from jax import lax
from jax.experimental import pallas as pl
from jax.experimental.pallas import tpu as pltpu
from jax.sharding import PartitionSpec as P

HEAD_DIM = 112
LANES = 128
SUBLANES = 8
CHUNKS = 2
MESH = pl.DeviceIdType.MESH


def split_heads(heads):
    count = min(CHUNKS, heads)
    base, extra = divmod(heads, count)
    chunks, first = [], 0
    for index in range(count):
        size = base + (1 if index < extra else 0)
        chunks.append((first, size))
        first += size
    return chunks


def two_terms(value):
    high = value.astype(jnp.bfloat16)
    low = (value - high.astype(jnp.float32)).astype(jnp.bfloat16)
    return high, low


def nn(a, b):
    return lax.dot_general(a, b, (((1,), (0,)), ((), ())), preferred_element_type=jnp.float32)


def nt(a, b):
    return lax.dot_general(a, b, (((1,), (1,)), ((), ())), preferred_element_type=jnp.float32)


def tn(a, b):
    return lax.dot_general(a, b, (((0,), (0,)), ((), ())), preferred_element_type=jnp.float32)


def kernel(
    n_space, n_tm, chunks, piece,
    q_ref, k_ref, v_ref, g_ref,
    mixed_ref, gq_ref, gk_ref, gv_ref,
    local, incoming, reduced, earlier, running, whole,
    rs_send, rs_recv, tm_send, tm_recv, ag_send, ag_recv,
):
    me = lax.axis_index("space")
    group = lax.axis_index("tm")
    rows = q_ref.shape[1]
    spare = LANES - HEAD_DIM
    columns = lax.broadcasted_iota(jnp.int32, (rows, spare), 1)

    barrier = pltpu.get_barrier_semaphore()
    for d in range(1, n_space):
        pl.semaphore_signal(
            barrier, inc=1, device_id={"space": lax.rem(me + d, n_space)}, device_id_type=MESH
        )
    for d in range(1, n_tm):
        pl.semaphore_signal(
            barrier, inc=1, device_id={"tm": lax.rem(group + d, n_tm)}, device_id_type=MESH
        )

    def head(ref, h):
        return ref[0, :, h * HEAD_DIM:(h + 1) * HEAD_DIM]

    def value_wide(h, ones):
        tail = jnp.where(columns < ones, 1.0, 0.0).astype(jnp.bfloat16)
        return jnp.concatenate([head(v_ref, h), tail], axis=1)

    def scatter_copy(phase, c, d):
        peer = lax.rem(me + d, n_space)
        return pltpu.make_async_remote_copy(
            src_ref=local.at[phase, c, pl.ds(pl.multiple_of(peer * piece, SUBLANES), piece)],
            dst_ref=incoming.at[phase, c, d - 1],
            send_sem=rs_send.at[phase, c, d - 1],
            recv_sem=rs_recv.at[phase, c, d - 1],
            device_id={"space": peer},
            device_id_type=MESH,
        )

    def group_copy(phase, c, d):
        peer = group + d if phase == 0 else group - d
        peer = jnp.clip(peer, 0, n_tm - 1)
        return pltpu.make_async_remote_copy(
            src_ref=reduced.at[phase, c],
            dst_ref=earlier.at[phase, c, d - 1],
            send_sem=tm_send.at[phase, c, d - 1],
            recv_sem=tm_recv.at[phase, c, d - 1],
            device_id={"tm": peer},
            device_id_type=MESH,
        )

    def gather_copy(phase, c, d):
        peer = lax.rem(me + d, n_space)
        return pltpu.make_async_remote_copy(
            src_ref=running.at[phase, c],
            dst_ref=whole.at[phase, c, pl.ds(pl.multiple_of(me * piece, SUBLANES), piece)],
            send_sem=ag_send.at[phase, c, d - 1],
            recv_sem=ag_recv.at[phase, c, d - 1],
            device_id={"space": peer},
            device_id_type=MESH,
        )

    def sends_to(phase, d):
        return group + d < n_tm if phase == 0 else group - d >= 0

    def hears_from(phase, d):
        return group - d >= 0 if phase == 0 else group + d < n_tm

    def scatter(phase, c):
        for d in range(1, n_space):
            scatter_copy(phase, c, d).start()

    def reduce(phase, c):
        total = local[phase, c, pl.ds(pl.multiple_of(me * piece, SUBLANES), piece)]
        for d in range(1, n_space):
            scatter_copy(phase, c, d).wait_recv()
            total = total + incoming[phase, c, d - 1]
        reduced[phase, c] = total
        running[phase, c] = total
        for d in range(1, n_tm):
            @pl.when(sends_to(phase, d))
            def _():
                group_copy(phase, c, d).start()

    def gather(phase, c):
        for d in range(1, n_tm):
            @pl.when(hears_from(phase, d))
            def _():
                group_copy(phase, c, d).wait_recv()
                running[phase, c] = running[phase, c] + earlier[phase, c, d - 1]
        for d in range(1, n_space):
            gather_copy(phase, c, d).start()
        whole[phase, c, pl.ds(pl.multiple_of(me * piece, SUBLANES), piece)] = running[phase, c]

    def arrive(phase, c):
        for d in range(1, n_space):
            gather_copy(phase, c, d).wait_recv()

    def pad(phase, c, size):
        spare_rows = n_space * piece - size * HEAD_DIM
        if spare_rows:
            local[phase, c, pl.ds(size * HEAD_DIM, spare_rows)] = jnp.zeros(
                (spare_rows, LANES), jnp.float32
            )

    def states(c):
        first, size = chunks[c]
        for i in range(size):
            h = first + i
            key_pos = jnp.maximum(head(k_ref, h), 0)
            local[0, c, pl.ds(i * HEAD_DIM, HEAD_DIM)] = tn(key_pos, value_wide(h, 2))
        pad(0, c, size)

    def queries(c):
        first, size = chunks[c]
        for i in range(size):
            h = first + i
            high, low = two_terms(whole[0, c, pl.ds(i * HEAD_DIM, HEAD_DIM)])
            query = head(q_ref, h)
            query_pos = jnp.maximum(query, 0)
            numer = nn(query_pos, high) + nn(query_pos, low)
            inverse = 1.0 / (numer[:, HEAD_DIM:HEAD_DIM + 1] + 1.0)
            attn = numer[:, :HEAD_DIM] * inverse
            mixed_ref[0, :, h * HEAD_DIM:(h + 1) * HEAD_DIM] = attn.astype(jnp.bfloat16)
            g_out = head(g_ref, h)
            g_wide = g_out.astype(jnp.float32)
            against = -jnp.sum(g_wide * attn, axis=1, keepdims=True)
            against_high, against_low = two_terms(against)
            tail = jnp.where(
                columns == 0,
                against_high.astype(jnp.float32),
                jnp.where(columns == 1, against_low.astype(jnp.float32), 0.0),
            ).astype(jnp.bfloat16)
            left = jnp.concatenate([g_out, tail], axis=1)
            feature = (nt(left, high) + nt(left, low)) * inverse
            gq_ref[0, :, h * HEAD_DIM:(h + 1) * HEAD_DIM] = jnp.where(
                query.astype(jnp.float32) > 0, feature, 0.0
            ).astype(jnp.bfloat16)
            right = jnp.concatenate(
                [g_wide, jnp.where(columns == 0, against, 0.0)], axis=1
            ) * inverse
            right_high, right_low = two_terms(right)
            local[1, c, pl.ds(i * HEAD_DIM, HEAD_DIM)] = tn(query_pos, right_high) + tn(
                query_pos, right_low
            )
        pad(1, c, size)

    def keys(c):
        first, size = chunks[c]
        for i in range(size):
            h = first + i
            high, low = two_terms(whole[1, c, pl.ds(i * HEAD_DIM, HEAD_DIM)])
            key = head(k_ref, h)
            key_pos = jnp.maximum(key, 0)
            value_gradient = nn(key_pos, high) + nn(key_pos, low)
            gv_ref[0, :, h * HEAD_DIM:(h + 1) * HEAD_DIM] = value_gradient[:, :HEAD_DIM].astype(
                jnp.bfloat16
            )
            value = value_wide(h, 1)
            key_gradient = nt(value, high) + nt(value, low)
            gk_ref[0, :, h * HEAD_DIM:(h + 1) * HEAD_DIM] = jnp.where(
                key.astype(jnp.float32) > 0, key_gradient, 0.0
            ).astype(jnp.bfloat16)

    count = len(chunks)
    for c in range(count):
        states(c)
        if c == 0:
            pl.semaphore_wait(barrier, n_space - 1 + n_tm - 1)
        scatter(0, c)
    for c in range(count):
        reduce(0, c)
    for c in range(count):
        gather(0, c)
    for c in range(count):
        arrive(0, c)
        queries(c)
        scatter(1, c)
    for c in range(count):
        reduce(1, c)
    for c in range(count):
        gather(1, c)
    for c in range(count):
        arrive(1, c)
        keys(c)
    for phase in range(2):
        for c in range(count):
            for d in range(1, n_space):
                scatter_copy(phase, c, d).wait_send()
                gather_copy(phase, c, d).wait_send()
            for d in range(1, n_tm):
                @pl.when(sends_to(phase, d))
                def _():
                    group_copy(phase, c, d).wait_send()


def solution(mesh):
    n_space, n_tm = mesh.shape["space"], mesh.shape["tm"]
    spec = P("tm", "space", None)

    def body(queries, keys_in, values_in, grad_attn):
        heads = queries.shape[2] // HEAD_DIM
        chunks = split_heads(heads)
        largest = max(size for _, size in chunks)
        piece = -(-largest * HEAD_DIM // (SUBLANES * n_space)) * SUBLANES
        count = len(chunks)
        vmem = pl.BlockSpec(memory_space=pltpu.VMEM)
        f32 = jnp.float32
        dma = pltpu.SemaphoreType.DMA
        peers, others = max(n_space - 1, 1), max(n_tm - 1, 1)
        return pl.pallas_call(
            functools.partial(kernel, n_space, n_tm, chunks, piece),
            out_shape=[jax.ShapeDtypeStruct(queries.shape, jnp.bfloat16)] * 4,
            in_specs=[vmem] * 4,
            out_specs=[vmem] * 4,
            scratch_shapes=[
                pltpu.VMEM((2, count, n_space * piece, LANES), f32),
                pltpu.VMEM((2, count, peers, piece, LANES), f32),
                pltpu.VMEM((2, count, piece, LANES), f32),
                pltpu.VMEM((2, count, others, piece, LANES), f32),
                pltpu.VMEM((2, count, piece, LANES), f32),
                pltpu.VMEM((2, count, n_space * piece, LANES), f32),
                dma((2, count, peers)),
                dma((2, count, peers)),
                dma((2, count, others)),
                dma((2, count, others)),
                dma((2, count, peers)),
                dma((2, count, peers)),
            ],
            compiler_params=pltpu.CompilerParams(collective_id=0, has_side_effects=True),
        )(queries, keys_in, values_in, grad_attn)

    return jax.shard_map(
        lambda *args: tuple(body(*args)),
        mesh=mesh,
        in_specs=(spec,) * 4,
        out_specs=(spec,) * 4,
        check_vma=False,
    )
```

```python
import functools

import jax
import jax.numpy as jnp
from jax import lax
from jax.experimental import pallas as pl
from jax.experimental.pallas import tpu as pltpu
from jax.sharding import PartitionSpec as P

HEAD_DIM = 112
LANES = 128
SUBLANES = 8
CHUNKS = 2
MESH = pl.DeviceIdType.MESH


def split_heads(heads):
    count = min(CHUNKS, heads)
    base, extra = divmod(heads, count)
    chunks, first = [], 0
    for index in range(count):
        size = base + (1 if index < extra else 0)
        chunks.append((first, size))
        first += size
    return chunks


def two_terms(value):
    high = value.astype(jnp.bfloat16)
    low = (value - high.astype(jnp.float32)).astype(jnp.bfloat16)
    return high, low


def nn(a, b):
    return lax.dot_general(a, b, (((1,), (0,)), ((), ())), preferred_element_type=jnp.float32)


def nt(a, b):
    return lax.dot_general(a, b, (((1,), (1,)), ((), ())), preferred_element_type=jnp.float32)


def tn(a, b):
    return lax.dot_general(a, b, (((0,), (0,)), ((), ())), preferred_element_type=jnp.float32)


def kernel(
    n_space, n_tm, chunks, piece,
    q_ref, k_ref, v_ref, g_ref,
    mixed_ref, gq_ref, gk_ref, gv_ref,
    local, incoming, reduced, earlier, running, whole,
    rs_send, rs_recv, tm_send, tm_recv, ag_send, ag_recv,
):
    me = lax.axis_index("space")
    group = lax.axis_index("tm")
    rows = q_ref.shape[2]
    spare = LANES - HEAD_DIM
    ids = lax.broadcasted_iota(jnp.int32, (spare, rows), 0)

    barrier = pltpu.get_barrier_semaphore()
    for d in range(1, n_space):
        pl.semaphore_signal(
            barrier, inc=1, device_id={"space": lax.rem(me + d, n_space)}, device_id_type=MESH
        )
    for d in range(1, n_tm):
        pl.semaphore_signal(
            barrier, inc=1, device_id={"tm": lax.rem(group + d, n_tm)}, device_id_type=MESH
        )

    def span(h):
        return pl.ds(h * HEAD_DIM, HEAD_DIM)

    def value_wide(h, ones):
        tail = jnp.where(ids < ones, 1.0, 0.0).astype(jnp.bfloat16)
        return jnp.concatenate([v_ref[0, span(h)], tail], axis=0)

    def scatter_copy(phase, c, d):
        peer = lax.rem(me + d, n_space)
        return pltpu.make_async_remote_copy(
            src_ref=local.at[phase, c, pl.ds(pl.multiple_of(peer * piece, SUBLANES), piece)],
            dst_ref=incoming.at[phase, c, d - 1],
            send_sem=rs_send.at[phase, c, d - 1],
            recv_sem=rs_recv.at[phase, c, d - 1],
            device_id={"space": peer},
            device_id_type=MESH,
        )

    def group_copy(phase, c, d):
        peer = group + d if phase == 0 else group - d
        peer = jnp.clip(peer, 0, n_tm - 1)
        return pltpu.make_async_remote_copy(
            src_ref=reduced.at[phase, c],
            dst_ref=earlier.at[phase, c, d - 1],
            send_sem=tm_send.at[phase, c, d - 1],
            recv_sem=tm_recv.at[phase, c, d - 1],
            device_id={"tm": peer},
            device_id_type=MESH,
        )

    def gather_copy(phase, c, d):
        peer = lax.rem(me + d, n_space)
        return pltpu.make_async_remote_copy(
            src_ref=running.at[phase, c],
            dst_ref=whole.at[phase, c, pl.ds(pl.multiple_of(me * piece, SUBLANES), piece)],
            send_sem=ag_send.at[phase, c, d - 1],
            recv_sem=ag_recv.at[phase, c, d - 1],
            device_id={"space": peer},
            device_id_type=MESH,
        )

    def sends_to(phase, d):
        return group + d < n_tm if phase == 0 else group - d >= 0

    def hears_from(phase, d):
        return group - d >= 0 if phase == 0 else group + d < n_tm

    def scatter(phase, c):
        for d in range(1, n_space):
            scatter_copy(phase, c, d).start()

    def reduce(phase, c):
        total = local[phase, c, pl.ds(pl.multiple_of(me * piece, SUBLANES), piece)]
        for d in range(1, n_space):
            scatter_copy(phase, c, d).wait_recv()
            total = total + incoming[phase, c, d - 1]
        reduced[phase, c] = total
        running[phase, c] = total
        for d in range(1, n_tm):
            @pl.when(sends_to(phase, d))
            def _():
                group_copy(phase, c, d).start()

    def gather(phase, c):
        for d in range(1, n_tm):
            @pl.when(hears_from(phase, d))
            def _():
                group_copy(phase, c, d).wait_recv()
                running[phase, c] = running[phase, c] + earlier[phase, c, d - 1]
        for d in range(1, n_space):
            gather_copy(phase, c, d).start()
        whole[phase, c, pl.ds(pl.multiple_of(me * piece, SUBLANES), piece)] = running[phase, c]

    def arrive(phase, c):
        for d in range(1, n_space):
            gather_copy(phase, c, d).wait_recv()

    def pad(phase, c, size):
        spare_rows = n_space * piece - size * HEAD_DIM
        if spare_rows:
            local[phase, c, pl.ds(size * HEAD_DIM, spare_rows)] = jnp.zeros(
                (spare_rows, LANES), jnp.float32
            )

    def states(c):
        first, size = chunks[c]
        for i in range(size):
            h = first + i
            key_pos = jnp.maximum(k_ref[0, span(h)], 0)
            local[0, c, span(i)] = nt(key_pos, value_wide(h, 2))
        pad(0, c, size)

    def queries(c):
        first, size = chunks[c]
        for i in range(size):
            h = first + i
            high, low = two_terms(whole[0, c, span(i)])
            query = q_ref[0, span(h)]
            query_pos = jnp.maximum(query, 0)
            numer = tn(jnp.concatenate([high, low], axis=0), jnp.concatenate([query_pos] * 2, axis=0))
            inverse = 1.0 / (numer[HEAD_DIM:HEAD_DIM + 1] + 1.0)
            attn = numer[:HEAD_DIM] * inverse
            mixed_ref[0, span(h)] = attn.astype(jnp.bfloat16)
            g_out = g_ref[0, span(h)]
            g_wide = g_out.astype(jnp.float32)
            against = -jnp.sum(g_wide * attn, axis=0, keepdims=True)
            against_high, against_low = two_terms(against)
            tail = jnp.where(
                ids == 0,
                against_high.astype(jnp.float32),
                jnp.where(ids == 1, against_low.astype(jnp.float32), 0.0),
            ).astype(jnp.bfloat16)
            feature = nn(
                jnp.concatenate([high, low], axis=1),
                jnp.concatenate([g_out, tail, g_out, tail], axis=0),
            ) * inverse
            gq_ref[0, span(h)] = jnp.where(
                query.astype(jnp.float32) > 0, feature, 0.0
            ).astype(jnp.bfloat16)
            right = jnp.concatenate([g_wide, jnp.where(ids == 0, against, 0.0)], axis=0) * inverse
            right_high, right_low = two_terms(right)
            local[1, c, span(i)] = nt(
                jnp.concatenate([query_pos] * 2, axis=1),
                jnp.concatenate([right_high, right_low], axis=1),
            )
        pad(1, c, size)

    def keys(c):
        first, size = chunks[c]
        for i in range(size):
            h = first + i
            high, low = two_terms(whole[1, c, span(i)])
            key = k_ref[0, span(h)]
            key_pos = jnp.maximum(key, 0)
            value_gradient = tn(
                jnp.concatenate([high, low], axis=0), jnp.concatenate([key_pos] * 2, axis=0)
            )
            gv_ref[0, span(h)] = value_gradient[:HEAD_DIM].astype(jnp.bfloat16)
            value = value_wide(h, 1)
            key_gradient = nn(
                jnp.concatenate([high, low], axis=1), jnp.concatenate([value, value], axis=0)
            )
            gk_ref[0, span(h)] = jnp.where(
                key.astype(jnp.float32) > 0, key_gradient, 0.0
            ).astype(jnp.bfloat16)

    count = len(chunks)
    for c in range(count):
        states(c)
        if c == 0:
            pl.semaphore_wait(barrier, n_space - 1 + n_tm - 1)
        scatter(0, c)
    for c in range(count):
        reduce(0, c)
    for c in range(count):
        gather(0, c)
    for c in range(count):
        arrive(0, c)
        queries(c)
        scatter(1, c)
    for c in range(count):
        reduce(1, c)
    for c in range(count):
        gather(1, c)
    for c in range(count):
        arrive(1, c)
        keys(c)
    for phase in range(2):
        for c in range(count):
            for d in range(1, n_space):
                scatter_copy(phase, c, d).wait_send()
                gather_copy(phase, c, d).wait_send()
            for d in range(1, n_tm):
                @pl.when(sends_to(phase, d))
                def _():
                    group_copy(phase, c, d).wait_send()


def solution(mesh):
    n_space, n_tm = mesh.shape["space"], mesh.shape["tm"]
    spec = P("tm", "space", None)

    def body(*args):
        args = [jnp.swapaxes(arg, 1, 2) for arg in args]
        heads = args[0].shape[1] // HEAD_DIM
        chunks = split_heads(heads)
        largest = max(size for _, size in chunks)
        piece = -(-largest * HEAD_DIM // (SUBLANES * n_space)) * SUBLANES
        count = len(chunks)
        vmem = pl.BlockSpec(memory_space=pltpu.VMEM)
        f32 = jnp.float32
        dma = pltpu.SemaphoreType.DMA
        peers, others = max(n_space - 1, 1), max(n_tm - 1, 1)
        outs = pl.pallas_call(
            functools.partial(kernel, n_space, n_tm, chunks, piece),
            out_shape=[jax.ShapeDtypeStruct(args[0].shape, jnp.bfloat16)] * 4,
            in_specs=[vmem] * 4,
            out_specs=[vmem] * 4,
            scratch_shapes=[
                pltpu.VMEM((2, count, n_space * piece, LANES), f32),
                pltpu.VMEM((2, count, peers, piece, LANES), f32),
                pltpu.VMEM((2, count, piece, LANES), f32),
                pltpu.VMEM((2, count, others, piece, LANES), f32),
                pltpu.VMEM((2, count, piece, LANES), f32),
                pltpu.VMEM((2, count, n_space * piece, LANES), f32),
                dma((2, count, peers)),
                dma((2, count, peers)),
                dma((2, count, others)),
                dma((2, count, others)),
                dma((2, count, peers)),
                dma((2, count, peers)),
            ],
            compiler_params=pltpu.CompilerParams(collective_id=0, has_side_effects=True),
        )(*args)
        return tuple(jnp.swapaxes(out, 1, 2) for out in outs)

    return jax.shard_map(
        body,
        mesh=mesh,
        in_specs=(spec,) * 4,
        out_specs=(spec,) * 4,
        check_vma=False,
    )
```

```python
import functools

import jax
import jax.numpy as jnp
from jax import lax
from jax.experimental import pallas as pl
from jax.experimental.pallas import tpu as pltpu
from jax.sharding import PartitionSpec as P

HEAD_DIM = 112
LANES = 128
SUBLANES = 8
CHUNKS = 2
VMEM_LIMIT = 24 * 1024 * 1024
MESH = pl.DeviceIdType.MESH


def split_heads(heads):
    count = min(CHUNKS, heads)
    base, extra = divmod(heads, count)
    chunks, first = [], 0
    for index in range(count):
        size = base + (1 if index < extra else 0)
        chunks.append((first, size))
        first += size
    return chunks


def two_terms(value):
    high = value.astype(jnp.bfloat16)
    low = (value - high.astype(jnp.float32)).astype(jnp.bfloat16)
    return high, low


def nn(a, b):
    return lax.dot_general(a, b, (((1,), (0,)), ((), ())), preferred_element_type=jnp.float32)


def nt(a, b):
    return lax.dot_general(a, b, (((1,), (1,)), ((), ())), preferred_element_type=jnp.float32)


def tn(a, b):
    return lax.dot_general(a, b, (((0,), (0,)), ((), ())), preferred_element_type=jnp.float32)


def kernel(
    n_space, n_tm, chunks, piece,
    q_ref, k_ref, v_ref, g_ref,
    mixed_ref, gq_ref, gk_ref, gv_ref,
    local, partner_half, half, incoming, reduced, earlier, running, whole,
    pair_send, pair_recv, rs_send, rs_recv, tm_send, tm_recv,
    ag_send, ag_recv, relay_send, relay_recv,
):
    me = lax.axis_index("space")
    group = lax.axis_index("tm")
    sites = n_space // 2
    site, side = lax.div(me, 2), lax.rem(me, 2)
    partner = me + 1 - 2 * side
    part = sites * piece
    rows = q_ref.shape[2]
    spare = LANES - HEAD_DIM
    ids = lax.broadcasted_iota(jnp.int32, (spare, rows), 0)

    def device(d):
        return 2 * lax.rem(site + d, sites) + side

    def rows_of(which, owner):
        start = which * part + owner * piece
        return pl.ds(pl.multiple_of(start, SUBLANES), piece)

    barrier = pltpu.get_barrier_semaphore()
    pl.semaphore_signal(barrier, inc=1, device_id={"space": partner}, device_id_type=MESH)
    for d in range(1, sites):
        pl.semaphore_signal(barrier, inc=1, device_id={"space": device(d)}, device_id_type=MESH)
    for d in range(1, n_tm):
        pl.semaphore_signal(
            barrier, inc=1, device_id={"tm": lax.rem(group + d, n_tm)}, device_id_type=MESH
        )

    def span(h):
        return pl.ds(h * HEAD_DIM, HEAD_DIM)

    def value_wide(h, ones):
        tail = jnp.where(ids < ones, 1.0, 0.0).astype(jnp.bfloat16)
        return jnp.concatenate([v_ref[0, span(h)], tail], axis=0)

    def pair_copy(phase, c):
        start = pl.multiple_of((1 - side) * part, SUBLANES)
        return pltpu.make_async_remote_copy(
            src_ref=local.at[phase, c, pl.ds(start, part)],
            dst_ref=partner_half.at[phase, c],
            send_sem=pair_send.at[phase, c],
            recv_sem=pair_recv.at[phase, c],
            device_id={"space": partner},
            device_id_type=MESH,
        )

    def scatter_copy(phase, c, d):
        owner = lax.rem(site + d, sites)
        return pltpu.make_async_remote_copy(
            src_ref=half.at[phase, c, pl.ds(pl.multiple_of(owner * piece, SUBLANES), piece)],
            dst_ref=incoming.at[phase, c, d - 1],
            send_sem=rs_send.at[phase, c, d - 1],
            recv_sem=rs_recv.at[phase, c, d - 1],
            device_id={"space": device(d)},
            device_id_type=MESH,
        )

    def group_copy(phase, c, d):
        peer = group + d if phase == 0 else group - d
        peer = jnp.clip(peer, 0, n_tm - 1)
        return pltpu.make_async_remote_copy(
            src_ref=reduced.at[phase, c],
            dst_ref=earlier.at[phase, c, d - 1],
            send_sem=tm_send.at[phase, c, d - 1],
            recv_sem=tm_recv.at[phase, c, d - 1],
            device_id={"tm": peer},
            device_id_type=MESH,
        )

    def gather_copy(phase, c, d):
        return pltpu.make_async_remote_copy(
            src_ref=running.at[phase, c],
            dst_ref=whole.at[phase, c, rows_of(side, site)],
            send_sem=ag_send.at[phase, c, d - 1],
            recv_sem=ag_recv.at[phase, c, d - 1],
            device_id={"space": device(d)},
            device_id_type=MESH,
        )

    def relay_copy(phase, c, d):
        rows = rows_of(side, lax.rem(site + sites - d, sites))
        return pltpu.make_async_remote_copy(
            src_ref=running.at[phase, c] if d == 0 else whole.at[phase, c, rows],
            dst_ref=whole.at[phase, c, rows],
            send_sem=relay_send.at[phase, c, d],
            recv_sem=relay_recv.at[phase, c, d],
            device_id={"space": partner},
            device_id_type=MESH,
        )

    def sends_to(phase, d):
        return group + d < n_tm if phase == 0 else group - d >= 0

    def hears_from(phase, d):
        return group - d >= 0 if phase == 0 else group + d < n_tm

    def exchange(phase, c):
        pair_copy(phase, c).start()

    def scatter(phase, c):
        pair_copy(phase, c).wait_recv()
        start = pl.multiple_of(side * part, SUBLANES)
        half[phase, c] = local[phase, c, pl.ds(start, part)] + partner_half[phase, c]
        for d in range(1, sites):
            scatter_copy(phase, c, d).start()

    def reduce(phase, c):
        total = half[phase, c, pl.ds(pl.multiple_of(site * piece, SUBLANES), piece)]
        for d in range(1, sites):
            scatter_copy(phase, c, d).wait_recv()
            total = total + incoming[phase, c, d - 1]
        reduced[phase, c] = total
        running[phase, c] = total
        for d in range(1, n_tm):
            @pl.when(sends_to(phase, d))
            def _():
                group_copy(phase, c, d).start()

    def gather(phase, c):
        for d in range(1, n_tm):
            @pl.when(hears_from(phase, d))
            def _():
                group_copy(phase, c, d).wait_recv()
                running[phase, c] = running[phase, c] + earlier[phase, c, d - 1]
        for d in range(1, sites):
            gather_copy(phase, c, d).start()
        relay_copy(phase, c, 0).start()
        whole[phase, c, rows_of(side, site)] = running[phase, c]

    def relay(phase, c):
        for d in range(1, sites):
            gather_copy(phase, c, d).wait_recv()
            relay_copy(phase, c, d).start()

    def arrive(phase, c):
        for d in range(sites):
            relay_copy(phase, c, d).wait_recv()

    def pad(phase, c, size):
        spare_rows = n_space * piece - size * HEAD_DIM
        if spare_rows:
            local[phase, c, pl.ds(size * HEAD_DIM, spare_rows)] = jnp.zeros(
                (spare_rows, LANES), jnp.float32
            )

    def states(c):
        first, size = chunks[c]
        for i in range(size):
            h = first + i
            key_pos = jnp.maximum(k_ref[0, span(h)], 0)
            local[0, c, span(i)] = nt(key_pos, value_wide(h, 2))
        pad(0, c, size)

    def queries(c):
        first, size = chunks[c]
        for i in range(size):
            h = first + i
            high, low = two_terms(whole[0, c, span(i)])
            query = q_ref[0, span(h)]
            query_pos = jnp.maximum(query, 0)
            numer = tn(jnp.concatenate([high, low], axis=0), jnp.concatenate([query_pos] * 2, axis=0))
            inverse = 1.0 / (numer[HEAD_DIM:HEAD_DIM + 1] + 1.0)
            attn = numer[:HEAD_DIM] * inverse
            mixed_ref[0, span(h)] = attn.astype(jnp.bfloat16)
            g_out = g_ref[0, span(h)]
            g_wide = g_out.astype(jnp.float32)
            against = -jnp.sum(g_wide * attn, axis=0, keepdims=True)
            against_high, against_low = two_terms(against)
            tail = jnp.where(
                ids == 0,
                against_high.astype(jnp.float32),
                jnp.where(ids == 1, against_low.astype(jnp.float32), 0.0),
            ).astype(jnp.bfloat16)
            feature = nn(
                jnp.concatenate([high, low], axis=1),
                jnp.concatenate([g_out, tail, g_out, tail], axis=0),
            ) * inverse
            gq_ref[0, span(h)] = jnp.where(
                query.astype(jnp.float32) > 0, feature, 0.0
            ).astype(jnp.bfloat16)
            right = jnp.concatenate([g_wide, jnp.where(ids == 0, against, 0.0)], axis=0) * inverse
            right_high, right_low = two_terms(right)
            local[1, c, span(i)] = nt(
                jnp.concatenate([query_pos] * 2, axis=1),
                jnp.concatenate([right_high, right_low], axis=1),
            )
        pad(1, c, size)

    def keys(c):
        first, size = chunks[c]
        for i in range(size):
            h = first + i
            high, low = two_terms(whole[1, c, span(i)])
            key = k_ref[0, span(h)]
            key_pos = jnp.maximum(key, 0)
            value_gradient = tn(
                jnp.concatenate([high, low], axis=0), jnp.concatenate([key_pos] * 2, axis=0)
            )
            gv_ref[0, span(h)] = value_gradient[:HEAD_DIM].astype(jnp.bfloat16)
            value = value_wide(h, 1)
            key_gradient = nn(
                jnp.concatenate([high, low], axis=1), jnp.concatenate([value, value], axis=0)
            )
            gk_ref[0, span(h)] = jnp.where(
                key.astype(jnp.float32) > 0, key_gradient, 0.0
            ).astype(jnp.bfloat16)

    count = len(chunks)
    for c in range(count):
        states(c)
        if c == 0:
            pl.semaphore_wait(barrier, 1 + sites - 1 + n_tm - 1)
        exchange(0, c)
    for phase, last in ((0, queries), (1, keys)):
        for c in range(count):
            scatter(phase, c)
        for c in range(count):
            reduce(phase, c)
        for c in range(count):
            gather(phase, c)
        for c in range(count):
            relay(phase, c)
        for c in range(count):
            arrive(phase, c)
            last(c)
            if phase == 0:
                exchange(1, c)
    for phase in range(2):
        for c in range(count):
            pair_copy(phase, c).wait_send()
            for d in range(1, sites):
                scatter_copy(phase, c, d).wait_send()
                gather_copy(phase, c, d).wait_send()
            for d in range(sites):
                relay_copy(phase, c, d).wait_send()
            for d in range(1, n_tm):
                @pl.when(sends_to(phase, d))
                def _():
                    group_copy(phase, c, d).wait_send()


def store(*refs):
    sources, targets, sems = refs[:4], refs[4:8], refs[8]
    copies = [
        pltpu.make_async_copy(source, target, sems.at[i])
        for i, (source, target) in enumerate(zip(sources, targets))
    ]
    for copy in copies:
        copy.start()
    for copy in copies:
        copy.wait()


def solution(mesh):
    n_space, n_tm = mesh.shape["space"], mesh.shape["tm"]
    spec = P("tm", "space", None)

    def body(*args):
        args = [jnp.swapaxes(arg, 1, 2) for arg in args]
        heads = args[0].shape[1] // HEAD_DIM
        chunks = split_heads(heads)
        largest = max(size for _, size in chunks)
        piece = -(-largest * HEAD_DIM // (SUBLANES * n_space)) * SUBLANES
        count = len(chunks)
        vmem = pl.BlockSpec(memory_space=pltpu.VMEM)
        f32 = jnp.float32
        dma = pltpu.SemaphoreType.DMA
        sites, others = n_space // 2, max(n_tm - 1, 1)
        peers = max(sites - 1, 1)
        outs = pl.pallas_call(
            functools.partial(kernel, n_space, n_tm, chunks, piece),
            out_shape=[pltpu.VMEM(args[0].shape, jnp.bfloat16)] * 4,
            in_specs=[vmem] * 4,
            out_specs=[vmem] * 4,
            scratch_shapes=[
                pltpu.VMEM((2, count, n_space * piece, LANES), f32),
                pltpu.VMEM((2, count, sites * piece, LANES), f32),
                pltpu.VMEM((2, count, sites * piece, LANES), f32),
                pltpu.VMEM((2, count, peers, piece, LANES), f32),
                pltpu.VMEM((2, count, piece, LANES), f32),
                pltpu.VMEM((2, count, others, piece, LANES), f32),
                pltpu.VMEM((2, count, piece, LANES), f32),
                pltpu.VMEM((2, count, n_space * piece, LANES), f32),
                dma((2, count)),
                dma((2, count)),
                dma((2, count, peers)),
                dma((2, count, peers)),
                dma((2, count, others)),
                dma((2, count, others)),
                dma((2, count, peers)),
                dma((2, count, peers)),
                dma((2, count, sites)),
                dma((2, count, sites)),
            ],
            compiler_params=pltpu.CompilerParams(
                collective_id=0, has_side_effects=True, vmem_limit_bytes=VMEM_LIMIT
            ),
        )(*args)
        anywhere = pl.BlockSpec(memory_space=pl.ANY)
        outs = pl.pallas_call(
            store,
            out_shape=[jax.ShapeDtypeStruct(args[0].shape, jnp.bfloat16)] * 4,
            in_specs=[vmem] * 4,
            out_specs=[anywhere] * 4,
            scratch_shapes=[dma((4,))],
            compiler_params=pltpu.CompilerParams(vmem_limit_bytes=VMEM_LIMIT),
        )(*outs)
        return tuple(jnp.swapaxes(out, 1, 2) for out in outs)

    return jax.shard_map(
        body,
        mesh=mesh,
        in_specs=(spec,) * 4,
        out_specs=(spec,) * 4,
        check_vma=False,
    )
```

```python
import functools

import jax
import jax.numpy as jnp
from jax import lax
from jax.experimental import pallas as pl
from jax.experimental.pallas import tpu as pltpu
from jax.sharding import PartitionSpec as P

HEAD_DIM = 112
LANES = 128
SUBLANES = 8
CHUNKS = 3
VMEM_LIMIT = 24 * 1024 * 1024
KERNEL_LIMIT = 65700000
DUE = (0.0, 2.0, 5.0, 8.5, 11.0, 12.5, 15.0, 18.0, 21.5, 24.0, 25.5)
SKEW = 1.2
MESH = pl.DeviceIdType.MESH


def split_heads(heads):
    count = min(CHUNKS, heads)
    base, extra = divmod(heads, count)
    chunks, first = [], 0
    for index in range(count):
        size = base + (1 if index < extra else 0)
        chunks.append((first, size))
        first += size
    return chunks


def two_terms(value):
    high = value.astype(jnp.bfloat16)
    low = (value - high.astype(jnp.float32)).astype(jnp.bfloat16)
    return high, low


def nn(a, b):
    return lax.dot_general(a, b, (((1,), (0,)), ((), ())), preferred_element_type=jnp.float32)


def nt(a, b):
    return lax.dot_general(a, b, (((1,), (1,)), ((), ())), preferred_element_type=jnp.float32)


def tn(a, b):
    return lax.dot_general(a, b, (((0,), (0,)), ((), ())), preferred_element_type=jnp.float32)


def kernel(
    n_space, n_tm, chunks, pieces,
    q_hbm, k_hbm, v_hbm, g_hbm,
    mixed_ref, gq_ref, gk_ref, gv_ref,
    q_ref, k_ref, v_ref, g_ref,
    local, partner_half, half, incoming, reduced, earlier, running, whole,
    pair_send, pair_recv, rs_send, rs_recv, tm_send, tm_recv,
    ag_send, ag_recv, relay_send, relay_recv, load_sem,
):
    me = lax.axis_index("space")
    group = lax.axis_index("tm")
    sites = n_space // 2
    site, side = lax.div(me, 2), lax.rem(me, 2)
    partner = me + 1 - 2 * side
    rows = q_ref.shape[2]
    spare = LANES - HEAD_DIM
    ids = lax.broadcasted_iota(jnp.int32, (spare, rows), 0)

    def device(d):
        return 2 * lax.rem(site + d, sites) + side

    def rows_of(c, which, owner):
        start = (which * sites + owner) * pieces[c]
        return pl.ds(pl.multiple_of(start, SUBLANES), pieces[c])

    def first_rows(c):
        return pl.ds(0, pieces[c])

    def half_rows(c):
        return pl.ds(0, sites * pieces[c])

    barrier = pltpu.get_barrier_semaphore()
    pl.semaphore_signal(barrier, inc=1, device_id={"space": partner}, device_id_type=MESH)
    for d in range(1, sites):
        pl.semaphore_signal(barrier, inc=1, device_id={"space": device(d)}, device_id_type=MESH)
    for d in range(1, n_tm):
        pl.semaphore_signal(
            barrier, inc=1, device_id={"tm": lax.rem(group + d, n_tm)}, device_id_type=MESH
        )

    def span(h):
        return pl.ds(h * HEAD_DIM, HEAD_DIM)

    def load(source, target, which, c):
        first, size = chunks[c]
        rows_in = pl.ds(first * HEAD_DIM, size * HEAD_DIM)
        return pltpu.make_async_copy(
            source.at[0, rows_in], target.at[0, rows_in], load_sem.at[which, c]
        )

    def value_wide(h, ones):
        tail = jnp.where(ids < ones, 1.0, 0.0).astype(jnp.bfloat16)
        return jnp.concatenate([v_ref[0, span(h)], tail], axis=0)

    def pair_copy(phase, c):
        part = sites * pieces[c]
        start = pl.multiple_of((1 - side) * part, SUBLANES)
        return pltpu.make_async_remote_copy(
            src_ref=local.at[phase, c, pl.ds(start, part)],
            dst_ref=partner_half.at[phase, c, half_rows(c)],
            send_sem=pair_send.at[phase, c],
            recv_sem=pair_recv.at[phase, c],
            device_id={"space": partner},
            device_id_type=MESH,
        )

    def scatter_copy(phase, c, d):
        owner = lax.rem(site + d, sites)
        return pltpu.make_async_remote_copy(
            src_ref=half.at[
                phase, c, pl.ds(pl.multiple_of(owner * pieces[c], SUBLANES), pieces[c])
            ],
            dst_ref=incoming.at[phase, c, d - 1, first_rows(c)],
            send_sem=rs_send.at[phase, c, d - 1],
            recv_sem=rs_recv.at[phase, c, d - 1],
            device_id={"space": device(d)},
            device_id_type=MESH,
        )

    def group_copy(phase, c, d):
        peer = group + d if phase == 0 else group - d
        peer = jnp.clip(peer, 0, n_tm - 1)
        return pltpu.make_async_remote_copy(
            src_ref=reduced.at[phase, c, first_rows(c)],
            dst_ref=earlier.at[phase, c, d - 1, first_rows(c)],
            send_sem=tm_send.at[phase, c, d - 1],
            recv_sem=tm_recv.at[phase, c, d - 1],
            device_id={"tm": peer},
            device_id_type=MESH,
        )

    def gather_copy(phase, c, d):
        return pltpu.make_async_remote_copy(
            src_ref=running.at[phase, c, first_rows(c)],
            dst_ref=whole.at[phase, c, rows_of(c, side, site)],
            send_sem=ag_send.at[phase, c, d - 1],
            recv_sem=ag_recv.at[phase, c, d - 1],
            device_id={"space": device(d)},
            device_id_type=MESH,
        )

    def relay_copy(phase, c, d):
        rows = rows_of(c, side, lax.rem(site + sites - d, sites))
        return pltpu.make_async_remote_copy(
            src_ref=running.at[phase, c, first_rows(c)] if d == 0 else whole.at[phase, c, rows],
            dst_ref=whole.at[phase, c, rows],
            send_sem=relay_send.at[phase, c, d],
            recv_sem=relay_recv.at[phase, c, d],
            device_id={"space": partner},
            device_id_type=MESH,
        )

    def sends_to(phase, d):
        return group + d < n_tm if phase == 0 else group - d >= 0

    def hears_from(phase, d):
        return group - d >= 0 if phase == 0 else group + d < n_tm

    def exchange(phase, c):
        pair_copy(phase, c).start()

    def scatter(phase, c):
        pair_copy(phase, c).wait_recv()
        part = sites * pieces[c]
        start = pl.multiple_of(side * part, SUBLANES)
        half[phase, c, half_rows(c)] = (
            local[phase, c, pl.ds(start, part)] + partner_half[phase, c, half_rows(c)]
        )
        for d in range(1, sites):
            scatter_copy(phase, c, d).start()

    def reduce(phase, c):
        total = half[phase, c, pl.ds(pl.multiple_of(site * pieces[c], SUBLANES), pieces[c])]
        for d in range(1, sites):
            scatter_copy(phase, c, d).wait_recv()
            total = total + incoming[phase, c, d - 1, first_rows(c)]
        reduced[phase, c, first_rows(c)] = total
        running[phase, c, first_rows(c)] = total
        for d in range(1, n_tm):
            @pl.when(sends_to(phase, d))
            def _():
                group_copy(phase, c, d).start()

    def gather(phase, c):
        for d in range(1, n_tm):
            @pl.when(hears_from(phase, d))
            def _():
                group_copy(phase, c, d).wait_recv()
                running[phase, c, first_rows(c)] = (
                    running[phase, c, first_rows(c)] + earlier[phase, c, d - 1, first_rows(c)]
                )
        for d in range(1, sites):
            gather_copy(phase, c, d).start()
        relay_copy(phase, c, 0).start()
        whole[phase, c, rows_of(c, side, site)] = running[phase, c, first_rows(c)]

    def relay(phase, c):
        for d in range(1, sites):
            gather_copy(phase, c, d).wait_recv()
            relay_copy(phase, c, d).start()

    def arrive(phase, c):
        for d in range(sites):
            relay_copy(phase, c, d).wait_recv()

    def pad(phase, c, size):
        spare_rows = n_space * pieces[c] - size * HEAD_DIM
        if spare_rows:
            local[phase, c, pl.ds(size * HEAD_DIM, spare_rows)] = jnp.zeros(
                (spare_rows, LANES), jnp.float32
            )

    def states(c):
        first, size = chunks[c]
        for i in range(size):
            h = first + i
            key_pos = jnp.maximum(k_ref[0, span(h)], 0)
            local[0, c, span(i)] = nt(key_pos, value_wide(h, 2))
        pad(0, c, size)

    def queries(c):
        first, size = chunks[c]
        for i in range(size):
            h = first + i
            high, low = two_terms(whole[0, c, span(i)])
            query = q_ref[0, span(h)]
            query_pos = jnp.maximum(query, 0)
            numer = tn(jnp.concatenate([high, low], axis=0), jnp.concatenate([query_pos] * 2, axis=0))
            inverse = 1.0 / (numer[HEAD_DIM:HEAD_DIM + 1] + 1.0)
            attn = numer[:HEAD_DIM] * inverse
            mixed_ref[0, span(h)] = attn.astype(jnp.bfloat16)
            g_out = g_ref[0, span(h)]
            g_wide = g_out.astype(jnp.float32)
            against = -jnp.sum(g_wide * attn, axis=0, keepdims=True)
            against_high, against_low = two_terms(against)
            tail = jnp.where(
                ids == 0,
                against_high.astype(jnp.float32),
                jnp.where(ids == 1, against_low.astype(jnp.float32), 0.0),
            ).astype(jnp.bfloat16)
            feature = nn(
                jnp.concatenate([high, low], axis=1),
                jnp.concatenate([g_out, tail, g_out, tail], axis=0),
            ) * inverse
            gq_ref[0, span(h)] = jnp.where(
                query.astype(jnp.float32) > 0, feature, 0.0
            ).astype(jnp.bfloat16)
            right = jnp.concatenate([g_wide, jnp.where(ids == 0, against, 0.0)], axis=0) * inverse
            right_high, right_low = two_terms(right)
            local[1, c, span(i)] = nt(
                jnp.concatenate([query_pos] * 2, axis=1),
                jnp.concatenate([right_high, right_low], axis=1),
            )
        pad(1, c, size)

    def keys(c):
        first, size = chunks[c]
        for i in range(size):
            h = first + i
            high, low = two_terms(whole[1, c, span(i)])
            key = k_ref[0, span(h)]
            key_pos = jnp.maximum(key, 0)
            value_gradient = tn(
                jnp.concatenate([high, low], axis=0), jnp.concatenate([key_pos] * 2, axis=0)
            )
            gv_ref[0, span(h)] = value_gradient[:HEAD_DIM].astype(jnp.bfloat16)
            value = value_wide(h, 1)
            key_gradient = nn(
                jnp.concatenate([high, low], axis=1), jnp.concatenate([value, value], axis=0)
            )
            gk_ref[0, span(h)] = jnp.where(
                key.astype(jnp.float32) > 0, key_gradient, 0.0
            ).astype(jnp.bfloat16)

    count = len(chunks)

    def start(c):
        if c == 0:
            for each in range(count):
                load(k_hbm, k_ref, 0, each).start()
                load(v_hbm, v_ref, 1, each).start()
            for each in range(count):
                load(q_hbm, q_ref, 2, each).start()
                load(g_hbm, g_ref, 3, each).start()
        load(k_hbm, k_ref, 0, c).wait()
        load(v_hbm, v_ref, 1, c).wait()
        states(c)
        if c == 0:
            pl.semaphore_wait(barrier, 1 + sites - 1 + n_tm - 1)
        exchange(0, c)

    def middle(c):
        arrive(0, c)
        load(q_hbm, q_ref, 2, c).wait()
        load(g_hbm, g_ref, 3, c).wait()
        queries(c)
        exchange(1, c)

    def finish(c):
        arrive(1, c)
        keys(c)

    stages = [start]
    for phase, last in ((0, middle), (1, finish)):
        for stage in (scatter, reduce, gather, relay):
            stages.append(functools.partial(stage, phase))
        stages.append(last)
    order = sorted(
        (DUE[s] + SKEW * c, s, c) for s in range(len(stages)) for c in range(count)
    )
    for _, s, c in order:
        stages[s](c)
    for phase in range(2):
        for c in range(count):
            pair_copy(phase, c).wait_send()
            for d in range(1, sites):
                scatter_copy(phase, c, d).wait_send()
                gather_copy(phase, c, d).wait_send()
            for d in range(sites):
                relay_copy(phase, c, d).wait_send()
            for d in range(1, n_tm):
                @pl.when(sends_to(phase, d))
                def _():
                    group_copy(phase, c, d).wait_send()


def store(*refs):
    sources, targets, sems = refs[:4], refs[4:8], refs[8]
    copies = [
        pltpu.make_async_copy(source, target, sems.at[i])
        for i, (source, target) in enumerate(zip(sources, targets))
    ]
    for copy in copies:
        copy.start()
    for copy in copies:
        copy.wait()


def solution(mesh):
    n_space, n_tm = mesh.shape["space"], mesh.shape["tm"]
    spec = P("tm", "space", None)

    def body(*args):
        args = [jnp.swapaxes(arg, 1, 2) for arg in args]
        heads = args[0].shape[1] // HEAD_DIM
        chunks = split_heads(heads)
        pieces = [-(-size * HEAD_DIM // (SUBLANES * n_space)) * SUBLANES for _, size in chunks]
        piece = max(pieces)
        count = len(chunks)
        vmem = pl.BlockSpec(memory_space=pltpu.VMEM)
        f32 = jnp.float32
        dma = pltpu.SemaphoreType.DMA
        sites, others = n_space // 2, max(n_tm - 1, 1)
        peers = max(sites - 1, 1)
        outs = pl.pallas_call(
            functools.partial(kernel, n_space, n_tm, chunks, pieces),
            out_shape=[pltpu.VMEM(args[0].shape, jnp.bfloat16)] * 4,
            in_specs=[pl.BlockSpec(memory_space=pltpu.HBM)] * 4,
            out_specs=[vmem] * 4,
            scratch_shapes=[pltpu.VMEM(args[0].shape, jnp.bfloat16)] * 4
            + [
                pltpu.VMEM((2, count, n_space * piece, LANES), f32),
                pltpu.VMEM((2, count, sites * piece, LANES), f32),
                pltpu.VMEM((2, count, sites * piece, LANES), f32),
                pltpu.VMEM((2, count, peers, piece, LANES), f32),
                pltpu.VMEM((2, count, piece, LANES), f32),
                pltpu.VMEM((2, count, others, piece, LANES), f32),
                pltpu.VMEM((2, count, piece, LANES), f32),
                pltpu.VMEM((2, count, n_space * piece, LANES), f32),
                dma((2, count)),
                dma((2, count)),
                dma((2, count, peers)),
                dma((2, count, peers)),
                dma((2, count, others)),
                dma((2, count, others)),
                dma((2, count, peers)),
                dma((2, count, peers)),
                dma((2, count, sites)),
                dma((2, count, sites)),
                dma((4, count)),
            ],
            compiler_params=pltpu.CompilerParams(
                collective_id=0, has_side_effects=True, vmem_limit_bytes=KERNEL_LIMIT
            ),
        )(*args)
        anywhere = pl.BlockSpec(memory_space=pl.ANY)
        outs = pl.pallas_call(
            store,
            out_shape=[jax.ShapeDtypeStruct(args[0].shape, jnp.bfloat16)] * 4,
            in_specs=[vmem] * 4,
            out_specs=[anywhere] * 4,
            scratch_shapes=[dma((4,))],
            compiler_params=pltpu.CompilerParams(vmem_limit_bytes=VMEM_LIMIT),
        )(*outs)
        return tuple(jnp.swapaxes(out, 1, 2) for out in outs)

    return jax.shard_map(
        body,
        mesh=mesh,
        in_specs=(spec,) * 4,
        out_specs=(spec,) * 4,
        check_vma=False,
    )
```
